32 devices in a mesh: expert: 8 (over z, x), hidden: 4 (over y, core).
Axes of the slice: x: 2, y: 2, z: 4, core: 2. Of those that a mesh axis runs over, the one named last changes fastest.
Arguments:
- pixels: bfloat16 [8192, 1024], P('expert', 'hidden'), may hold values from -6 to 6
- conv_weight: float32 [9, 1024], P(None, 'hidden'), may hold values from -2.5 to 2.5
- norm_gain: float32 [1024], replicated, may hold values from 0.1 to 1.9
- router_weight: bfloat16 [1024, 8], P(None, 'expert'), may hold values from -0.375 to 0.375
- gate_weight: bfloat16 [8, 1024, 4096], P('expert', None, 'hidden'), may hold values from -0.1875 to 0.1875
- up_weight: bfloat16 [8, 1024, 4096], P('expert', None, 'hidden'), may hold values from -0.1875 to 0.1875
- down_weight: bfloat16 [8, 4096, 1024], P('expert', 'hidden'), may hold values from -0.09375 to 0.09375
- expert_ids: int32 [8192, 1], P('expert'), may hold values from 0 to 7; in each aligned block of 1024 rows (0 to 1023, 1024 to 2047, ...) at most 256 rows name the same one
- neighbours: int32 [8, 8], P('expert'), may hold values from -1 to 7, as said below
Outputs:
- block_out: bfloat16 [8192, 1024], P('expert', 'hidden')
The draws below stay inside these ranges and needn't reach their ends.
Inputs may be any that keep to these rules, and one draw needn't show every extreme that they name: `expert_ids`: among the 1024 pixels of one tile (the rows of one device) no expert is named more than 256 times. `neighbours`: A simplified stand-in for the sphere's tile adjacency: the tiles form a grid of 2 rows by 4 columns that closes in the columns; row t lists the tiles to the north, south, west, east, northwest, northeast, southwest and southeast of tile t, and -1 stands for a place beyond the first or last grid row. Which tile stands where is arbitrary.
All inputs are finite; a program needn't handle non-finite values.
Results may differ from the reference program's by a relative error of at most 0.0055.
Values may be sent and summed in bfloat16 or wider, within the bound.
No kernel may reach another device: no remote copies, remote signals or barrier semaphores. Data moves between devices by JAX's collectives and lax.ppermute only.
A program may use at most 128 MiB of HBM per device.

```python
import math
import jax
import jax.numpy as jnp
import numpy as np
from jax import lax

D = 1024
FF = 4096
TILE_SIDE = 32
TOK_DEV = 1024
EXPERTS = 8
TILES = 8
PIXELS = 8192
CAP = 256


def draw_neighbours(key, part):
    grid_rows = TILES // 4
    tile_order = jax.random.permutation(key, TILES).astype(jnp.int32)
    position = jnp.arange(TILES, dtype=jnp.int32)
    grid_row = position // 4
    grid_col = position % 4
    offsets = [(-1, 0), (1, 0), (0, -1), (0, 1), (-1, -1), (-1, 1), (1, -1), (1, 1)]
    columns = []
    for row_step, col_step in offsets:
        next_row = grid_row + row_step
        next_col = (grid_col + col_step) % 4
        inside = (next_row >= 0) & (next_row < grid_rows)
        spot = jnp.clip(next_row, 0, grid_rows - 1) * 4 + next_col
        columns.append(jnp.where(inside, tile_order[spot], -1))
    stacked = jnp.stack(columns, axis=1).astype(jnp.int32)
    return jnp.zeros((TILES, 8), jnp.int32).at[tile_order].set(stacked)


def block_levels(rng, shape, cuts, low, largest):
    factor_of = 1.0
    for dim, blocks in cuts:
        draws = jax.random.uniform(jax.random.fold_in(jax.random.fold_in(rng, 6), dim), (blocks,), jnp.float32, low / len(cuts), largest / len(cuts))
        factor_of = factor_of * jnp.repeat(jnp.exp(draws), shape[dim] // blocks).reshape((-1,) + (1,) * (len(shape) - 1 - dim))
    return factor_of


def shared_out(own_key, own, number, rows, number_of, top, limit, skew):
    order = jax.random.permutation(own_key, number_of)
    crowded, usual = shares(number_of, rows * top, limit, skew, True), shares(number_of, rows * top, limit, skew, False)
    places = jnp.arange(number_of)

    def named(lengths, offset_by):
        used = int((lengths > 0).sum())
        fixed = max(1, used // 4)
        moved = fixed + (places - fixed + offset_by * (used - fixed)) % max(1, number_of - fixed)
        return jnp.zeros((number_of,), jnp.int32).at[order[jnp.where(places < fixed, places, moved)]].set(jnp.asarray(lengths, jnp.int32))

    lengths = jnp.where(number % 4 == 0, named(crowded, number // 4), named(usual, number - number // 4 - 1))
    mixed = jax.random.permutation(jax.random.fold_in(own, 3), number_of)
    source_of, taker = mixed[0:number_of // 2 * 2:2], mixed[1:number_of // 2 * 2:2]
    margin = jnp.minimum(lengths[source_of] - 1, limit - lengths[taker]) // 2
    margin = jnp.where((source_of == order[0]) | (taker == order[0]) | (lengths[taker] == 0), 0, jnp.maximum(margin, 0))
    moved = jax.random.randint(jax.random.fold_in(own, 4), (number_of // 2,), 0, 1 << 20) % (margin + 1)
    lengths = lengths.at[source_of].add(-moved).at[taker].add(moved)
    members = jnp.searchsorted(jnp.cumsum(lengths), jnp.arange(rows * top), side="right").astype(jnp.int32)
    listing = members.reshape(top, rows).T
    listing = listing[jax.random.permutation(jax.random.fold_in(own, 1), rows)]
    offset_by = jax.random.randint(jax.random.fold_in(own, 2), (rows, 1), 0, top)
    return jnp.take_along_axis(listing, (jnp.arange(top)[None, :] + offset_by) % top, axis=1)


def shares(number_of, total, most, skew, full):
    loads = [(1 << 20) // math.isqrt(grade ** skew) + 1 for grade in range(1, number_of + 1)]
    largest = most if full else min(most, max(-(-total // number_of), total * loads[0] // sum(loads)))
    least = 1 if total - largest >= number_of - 1 else 0
    given, surplus = [largest] + [least] * (number_of - 1), total - largest - least * (number_of - 1)
    while surplus > 0:
        candidates = [i for i in range(1, number_of) if given[i] < largest] or [i for i in range(1, number_of) if given[i] < most]
        mass, budget = sum([loads[i] for i in candidates]), surplus
        for i in candidates:
            addition = min(most - given[i], max(1, budget * loads[i] // mass), surplus)
            given[i] = given[i] + addition
            surplus = surplus - addition
    return np.array(given)


def gaussian(own_key, dims, width, most, cuts=(), kind=jnp.bfloat16):
    values = jax.random.normal(own_key, dims, jnp.float32) * width
    if len(cuts) > 0:
        values = block_levels(own_key, dims, cuts, -0.22, 0.18) * values
    return jnp.clip(values, min=-most, max=most).astype(kind)


def setup_inputs(seed: int = 0) -> dict:
    key_of = jax.random.split(jax.random.key(seed), 10)
    pixels = gaussian(key_of[0], (PIXELS, D), 1.0, 6.0, ((0, 8), (1, 4)))
    conv_weight = gaussian(key_of[1], (9, D), 0.35, 2.5, ((1, 4),), jnp.float32)
    norm_gain = jnp.clip(1.0 + 0.18 * jax.random.normal(key_of[2], (D,), jnp.float32), 0.1, 1.9)
    router_weight = gaussian(key_of[3], (D, EXPERTS), (D // 4) ** -0.5, 0.375, ((1, 8),))
    gate_weight = gaussian(key_of[4], (EXPERTS, D, FF), D ** -0.5, 0.1875, ((0, 8), (2, 4)))
    up_weight = gaussian(key_of[5], (EXPERTS, D, FF), D ** -0.5, 0.1875, ((0, 8), (2, 4)))
    down_weight = gaussian(key_of[6], (EXPERTS, FF, D), FF ** -0.5, 0.09375, ((0, 8), (1, 4)))
    expert_ids_keys = jax.random.split(jax.random.fold_in(key_of[7], 1), PIXELS // TOK_DEV)
    expert_ids_turns = jax.random.permutation(jax.random.fold_in(key_of[7], 3), PIXELS // TOK_DEV)
    expert_ids = jax.vmap(lambda own, number: shared_out(jax.random.fold_in(key_of[7], 2), own, number, TOK_DEV, EXPERTS, 1, CAP, 2))(expert_ids_keys, expert_ids_turns).reshape((PIXELS, 1))
    neighbours = draw_neighbours(jax.random.fold_in(key_of[9], 71), 0)
    return dict(pixels=pixels, conv_weight=conv_weight, norm_gain=norm_gain, router_weight=router_weight, gate_weight=gate_weight, up_weight=up_weight, down_weight=down_weight, expert_ids=expert_ids, neighbours=neighbours)


epsilon = 1e-05

def reference(pixels, conv_weight, norm_gain, router_weight, gate_weight, up_weight, down_weight, expert_ids, neighbours):
    tile_side = TILE_SIDE
    tiles = pixels.astype(jnp.float32).reshape(TILES, tile_side, tile_side, D)
    present = (neighbours >= 0).astype(jnp.float32)
    source_tile = jnp.maximum(neighbours, 0).astype(jnp.int32)

    def fetch_rim(edge, direction):
        picked = edge[source_tile[:, direction]]
        return picked * present[:, direction].reshape((TILES,) + (1,) * (edge.ndim - 1))
    north = fetch_rim(tiles[:, tile_side - 1], 0)
    south = fetch_rim(tiles[:, 0], 1)
    west = fetch_rim(tiles[:, :, tile_side - 1], 2)
    east = fetch_rim(tiles[:, :, 0], 3)
    corner_nw = fetch_rim(tiles[:, tile_side - 1, tile_side - 1], 4)
    corner_ne = fetch_rim(tiles[:, tile_side - 1, 0], 5)
    corner_sw = fetch_rim(tiles[:, 0, tile_side - 1], 6)
    corner_se = fetch_rim(tiles[:, 0, 0], 7)
    upper_rim = jnp.concatenate([corner_nw[:, None], north, corner_ne[:, None]], axis=1)
    lower_rim = jnp.concatenate([corner_sw[:, None], south, corner_se[:, None]], axis=1)
    middle = jnp.concatenate([west[:, :, None], tiles, east[:, :, None]], axis=2)
    padded = jnp.concatenate([upper_rim[:, None], middle, lower_rim[:, None]], axis=1)
    mixed = tiles
    for row_off in range(3):
        for col_off in range(3):
            mixed = mixed + conv_weight[3 * row_off + col_off] * padded[:, row_off:row_off + tile_side, col_off:col_off + tile_side]
    conv_out = mixed.astype(jnp.bfloat16).reshape(PIXELS, D)
    wide_feats = conv_out.astype(jnp.float32)
    mean_sq = lax.optimization_barrier(jnp.mean(wide_feats * wide_feats, axis=1, keepdims=True))
    normed = (wide_feats * lax.rsqrt(mean_sq + epsilon) * norm_gain).astype(jnp.bfloat16)
    expert_of = expert_ids[:, 0].astype(jnp.int32)
    onehot = (expert_of[:, None] == jnp.arange(EXPERTS, dtype=jnp.int32)[None]).astype(jnp.int32)
    onehot = onehot.reshape(TILES, TOK_DEV, EXPERTS)
    ranks = jnp.cumsum(onehot, axis=1) - onehot
    slot_index = lax.optimization_barrier(jnp.sum(ranks * onehot, axis=2)).reshape(PIXELS).astype(jnp.int32)
    tile_of = (jnp.arange(PIXELS, dtype=jnp.int32) // TOK_DEV).astype(jnp.int32)
    position = (tile_of * CAP + slot_index).astype(jnp.int32)
    logits = jnp.dot(normed, router_weight, preferred_element_type=jnp.float32)
    weight = jax.nn.sigmoid(jnp.take_along_axis(logits, expert_of[:, None], axis=1))
    buffer_rows = TILES * CAP

    def per_expert(accum, expert_index):
        routed = expert_of == expert_index
        target = jnp.where(routed, position, buffer_rows).astype(jnp.int32)
        buffer = jnp.zeros((buffer_rows, D), jnp.bfloat16).at[target].set(normed, mode='drop')
        gate_buffer = jnp.zeros((buffer_rows, 1), jnp.float32).at[target].set(weight, mode='drop')
        gate_act = jnp.dot(buffer, gate_weight[expert_index], preferred_element_type=jnp.float32)
        up_act = jnp.dot(buffer, up_weight[expert_index], preferred_element_type=jnp.float32)
        hidden = (jax.nn.silu(gate_act) * up_act * gate_buffer).astype(jnp.bfloat16)
        result = jnp.dot(hidden, down_weight[expert_index], preferred_element_type=jnp.float32).astype(jnp.bfloat16)
        fetched = result[jnp.minimum(target, buffer_rows - 1)].astype(jnp.float32)
        accum = accum + jnp.where(routed[:, None], fetched, jnp.zeros_like(fetched))
        return (accum, None)
    expert_sum, unused = lax.scan(per_expert, jnp.zeros((PIXELS, D), jnp.float32), jnp.arange(EXPERTS, dtype=jnp.int32))
    return (conv_out.astype(jnp.float32) + expert_sum).astype(jnp.bfloat16)
```

```python
import functools

import jax
import jax.numpy as jnp
from jax import lax
from jax.experimental import pallas as pl
from jax.experimental.pallas import tpu as pltpu
from jax.sharding import PartitionSpec as P

SIDE = 32
EPSILON = 1e-05
CHUNKS = 2

f32 = jnp.float32
bf16 = jnp.bfloat16

VMEM = pltpu.MemorySpace.VMEM
SMEM = pltpu.MemorySpace.SMEM


def whole_vmem():
    return pl.BlockSpec(memory_space=VMEM)


def whole_smem():
    return pl.BlockSpec(memory_space=SMEM)


def params(mib):
    return pltpu.CompilerParams(vmem_limit_bytes=mib << 20)


def rim_kernel(nbr_ref, pix_ref, out_ref):
    tokens = pix_ref.shape[0]
    out_ref[...] = jnp.zeros_like(out_ref)
    last = tokens - SIDE
    line = lax.broadcasted_iota(jnp.int32, (2 * SIDE, tokens), 0)
    pixel = lax.broadcasted_iota(jnp.int32, (2 * SIDE, tokens), 1)
    wanted = jnp.where(line < SIDE, line * SIDE, (line - SIDE) * SIDE + SIDE - 1)
    pick = jnp.where(pixel == wanted, 1.0, 0.0).astype(bf16)
    columns = jnp.dot(pick, pix_ref[...], preferred_element_type=f32)

    def put(direction, piece):
        target = nbr_ref[0, direction]

        @pl.when(target >= 0)
        def _():
            out_ref[jnp.maximum(target, 0), : piece.shape[0], :] = piece

    put(0, pix_ref[:SIDE])
    put(1, pix_ref[last:])
    put(2, columns[:SIDE].astype(bf16))
    put(3, columns[SIDE:].astype(bf16))
    for direction, row in ((4, 0), (5, SIDE), (6, SIDE - 1), (7, 2 * SIDE - 1)):
        corner = columns[row : row + 1, :]
        put(direction, jnp.broadcast_to(corner, (16, corner.shape[1])).astype(bf16))


def rim_send(neighbours, pixels, experts):
    tokens, width = pixels.shape
    return pl.pallas_call(
        rim_kernel,
        out_shape=jax.ShapeDtypeStruct((experts, SIDE, width), bf16),
        in_specs=[whole_smem(), whole_vmem()],
        out_specs=whole_vmem(),
        compiler_params=params(8),
        name="rim_send",
    )(neighbours, pixels)


def shifted_rows(pix_ref, side_ref):
    tokens = pix_ref.shape[0]
    wide = pix_ref[...].astype(f32)
    side_ref[1, SIDE : SIDE + tokens, :] = wide
    side_ref[0, SIDE : SIDE + tokens, :] = pltpu.roll(wide, 1, 0)
    side_ref[2, SIDE : SIDE + tokens, :] = pltpu.roll(wide, tokens - 1, 0)


def conv_rows(side_ref, weight_ref, conv_ref):
    tokens = conv_ref.shape[0]
    step = 64

    def block(number, carry):
        start = pl.multiple_of(number * step, step)
        total = side_ref[1, pl.ds(start + SIDE, step), :]
        for a in range(3):
            for b in range(3):
                total = (
                    total
                    + weight_ref[3 * a + b : 3 * a + b + 1, :]
                    * side_ref[b, pl.ds(start + SIDE * a, step), :]
                )
        conv_ref[pl.ds(start, step), :] = total.astype(bf16)
        return carry

    lax.fori_loop(0, tokens // step, block, 0)


def send_rows(pos_row, conv, out_ref):
    rows = out_ref.shape[0]
    tokens = conv.shape[0]
    step = min(256, rows)
    for start in range(0, rows, step):
        slots = lax.broadcasted_iota(jnp.int32, (step, tokens), 0) + start
        pick = jnp.where(slots == pos_row, 1.0, 0.0).astype(bf16)
        out_ref[start : start + step, :] = jnp.dot(
            pick, conv, preferred_element_type=f32
        ).astype(bf16)


def route(ids_row, experts, capacity, chunks, split_border):
    tokens = ids_row.shape[1]
    token = lax.broadcasted_iota(jnp.int32, (1, tokens), 1)
    if split_border:
        i, j = token // SIDE, token % SIDE
        border = (i == 0) | (i == SIDE - 1) | (j == 0) | (j == SIDE - 1)
        kind = jnp.where(border, ids_row + experts, ids_row)
        kinds = 2 * experts
    else:
        kind, kinds = ids_row, experts
    onehot = jnp.where(lax.broadcasted_iota(jnp.int32, (kinds, tokens), 0) == kind, 1.0, 0.0)
    before = jnp.where(
        lax.broadcasted_iota(jnp.int32, (tokens, tokens), 0)
        < lax.broadcasted_iota(jnp.int32, (tokens, tokens), 1),
        1.0,
        0.0,
    ).astype(bf16)
    earlier = jnp.dot(onehot.astype(bf16), before, preferred_element_type=f32)
    slot = jnp.sum(onehot * earlier, axis=0, keepdims=True).astype(jnp.int32)
    if split_border:
        slot = jnp.where(border, capacity - 1 - slot, slot)
    size = capacity // chunks
    result = []
    for chunk in range(chunks):
        low = chunk * size
        inside = (slot >= low) & (slot < low + size)
        result.append(jnp.where(inside, ids_row * size + slot - low, -1))
    return result


def early_kernel(
    ids_ref, pix_ref, weight_ref, pos_ref, out_ref, side_ref, conv_ref, *, experts, capacity, chunks
):
    positions = route(ids_ref[...], experts, capacity, chunks, True)
    for chunk in range(chunks):
        pos_ref[chunk : chunk + 1, :] = positions[chunk]
    tokens, width = pix_ref.shape
    shifted_rows(pix_ref, side_ref)
    for b in range(3):
        side_ref[b, :SIDE, :] = jnp.zeros((SIDE, width), f32)
        side_ref[b, SIDE + tokens :, :] = jnp.zeros((SIDE, width), f32)
    conv_rows(side_ref, weight_ref, conv_ref)
    send_rows(positions[0], conv_ref[...], out_ref)


def early(ids_row, pixels, conv_weight, experts, capacity, chunks):
    tokens, width = pixels.shape
    rows = experts * capacity // chunks
    return pl.pallas_call(
        functools.partial(early_kernel, experts=experts, capacity=capacity, chunks=chunks),
        out_shape=(
            jax.ShapeDtypeStruct((chunks, tokens), jnp.int32),
            jax.ShapeDtypeStruct((rows, width), bf16),
        ),
        in_specs=[whole_vmem()] * 3,
        out_specs=(whole_vmem(), whole_vmem()),
        scratch_shapes=[
            pltpu.VMEM((3, tokens + 2 * SIDE, width), f32),
            pltpu.VMEM((tokens, width), bf16),
        ],
        compiler_params=params(24),
        name="early",
    )(ids_row, pixels, conv_weight)


def route_kernel(ids_ref, pos_ref, *, experts, capacity, chunks):
    positions = route(ids_ref[...], experts, capacity, chunks, False)
    for chunk in range(chunks):
        pos_ref[chunk : chunk + 1, :] = positions[chunk]


def route_only(ids_row, experts, capacity, chunks):
    return pl.pallas_call(
        functools.partial(route_kernel, experts=experts, capacity=capacity, chunks=chunks),
        out_shape=jax.ShapeDtypeStruct((chunks, ids_row.shape[1]), jnp.int32),
        in_specs=[whole_vmem()],
        out_specs=whole_vmem(),
        compiler_params=params(16),
        name="route",
    )(ids_row)


def late_kernel(nbr_ref, pos_ref, pix_ref, weight_ref, rim_ref, conv_ref, *rest, first):
    outs, side_ref = rest[:-1], rest[-1]
    tokens, width = pix_ref.shape
    shifted_rows(pix_ref, side_ref)

    def fetch(direction):
        source = nbr_ref[0, direction]
        block = rim_ref[jnp.maximum(source, 0)].astype(f32)
        return jnp.where(source >= 0, block, 0.0)

    pixel = lax.broadcasted_iota(jnp.int32, (tokens, SIDE), 0)
    line = lax.broadcasted_iota(jnp.int32, (tokens, SIDE), 1)
    column = lax.broadcasted_iota(jnp.int32, (tokens, width), 0) % SIDE
    for b, direction, edge in ((0, 2, 0), (2, 3, SIDE - 1)):
        place = jnp.where(pixel == line * SIDE + edge, 1.0, 0.0).astype(bf16)
        values = jnp.dot(place, fetch(direction).astype(bf16), preferred_element_type=f32)
        inner = side_ref[b, SIDE : SIDE + tokens, :]
        side_ref[b, SIDE : SIDE + tokens, :] = jnp.where(column == edge, values, inner)
    place = lax.broadcasted_iota(jnp.int32, (SIDE, width), 0)
    for middle, left, right, start in ((0, 4, 5, 0), (1, 6, 7, SIDE + tokens)):
        row = fetch(middle)
        side_ref[1, start : start + SIDE, :] = row
        side_ref[0, start : start + SIDE, :] = jnp.where(
            place == 0, fetch(left)[0:1, :], pltpu.roll(row, 1, 0)
        )
        side_ref[2, start : start + SIDE, :] = jnp.where(
            place == SIDE - 1, fetch(right)[0:1, :], pltpu.roll(row, SIDE - 1, 0)
        )
    conv_rows(side_ref, weight_ref, conv_ref)
    for number, out_ref in enumerate(outs):
        chunk = first + number
        send_rows(pos_ref[chunk : chunk + 1, :], conv_ref[...], out_ref)


def late(neighbours, positions, pixels, conv_weight, rim, first, rows):
    tokens, width = pixels.shape
    left = positions.shape[0] - first
    return pl.pallas_call(
        functools.partial(late_kernel, first=first),
        out_shape=(jax.ShapeDtypeStruct((tokens, width), bf16),)
        + (jax.ShapeDtypeStruct((rows, width), bf16),) * left,
        in_specs=[whole_smem()] + [whole_vmem()] * 4,
        out_specs=(whole_vmem(),) * (left + 1),
        scratch_shapes=[pltpu.VMEM((3, tokens + 2 * SIDE, width), f32)],
        compiler_params=params(24),
        name="late",
    )(neighbours, positions, pixels, conv_weight, rim)


def expert_kernel(
    own_ref,
    x0_ref,
    x1_ref,
    x2_ref,
    x3_ref,
    gain_ref,
    router_ref,
    gate_ref,
    up_ref,
    down_ref,
    keep0_ref,
    keep1_ref,
    give_ref,
    normed_ref,
):
    own = own_ref[0]
    pieces = (x0_ref, x1_ref, x2_ref, x3_ref)
    order = (own, own ^ 2, own ^ 1, own ^ 3)
    width = x0_ref.shape[1]
    square = 0.0
    for piece in pieces:
        wide = piece[...].astype(f32)
        square = square + wide * wide
    mean_sq = jnp.sum(square, axis=1, keepdims=True) * (1.0 / (width * len(pieces)))
    scale = lax.rsqrt(mean_sq + EPSILON)
    score = 0.0
    for piece, part in zip(pieces, order):
        normed = (piece[...].astype(f32) * scale * gain_ref[part]).astype(bf16)
        score = score + normed.astype(f32) * router_ref[part]
        start = pl.multiple_of(part * width, width)
        normed_ref[:, pl.ds(start, width)] = normed
    weight = jax.nn.sigmoid(jnp.sum(score, axis=1, keepdims=True))
    rows = normed_ref[...]
    gate = jnp.dot(rows, gate_ref[0], preferred_element_type=f32)
    up = jnp.dot(rows, up_ref[0], preferred_element_type=f32)
    hidden = (gate / (1.0 + jnp.exp(-gate)) * up * weight).astype(bf16)

    def columns(part):
        start = pl.multiple_of(part * width, width)
        return jnp.dot(
            hidden, down_ref[0, :, pl.ds(start, width)], preferred_element_type=f32
        ).astype(bf16)

    keep0_ref[...] = columns(order[0])
    keep1_ref[...] = columns(order[1])
    give_ref[0] = columns(order[2])
    give_ref[1] = columns(order[3])


def expert_layer(own, pieces, gain, router, gate_weight, up_weight, down_weight):
    rows, width = pieces[0].shape
    step = min(256, rows)
    x_spec = pl.BlockSpec((step, width), lambda i: (i, 0))

    def fixed(shape):
        return pl.BlockSpec(shape, lambda i: (0,) * len(shape))

    full = gate_weight.shape[1]
    return pl.pallas_call(
        expert_kernel,
        grid=(rows // step,),
        out_shape=(
            jax.ShapeDtypeStruct((rows, width), bf16),
            jax.ShapeDtypeStruct((rows, width), bf16),
            jax.ShapeDtypeStruct((2, rows, width), bf16),
        ),
        in_specs=[whole_smem()]
        + [x_spec] * 4
        + [
            fixed(gain.shape),
            fixed(router.shape),
            fixed(gate_weight.shape),
            fixed(up_weight.shape),
            fixed(down_weight.shape),
        ],
        out_specs=(x_spec, x_spec, pl.BlockSpec((2, step, width), lambda i: (0, i, 0))),
        scratch_shapes=[pltpu.VMEM((step, full), bf16)],
        compiler_params=params(40),
        cost_estimate=pl.CostEstimate(
            flops=6 * rows * full * gate_weight.shape[2],
            transcendentals=rows * gate_weight.shape[2],
            bytes_accessed=3 * 2 * full * gate_weight.shape[2] + 4 * rows * full,
        ),
        name="expert",
    )(own, *pieces, gain, router, gate_weight, up_weight, down_weight)


def combine_kernel(pos_ref, base_ref, rows_ref, out_ref, *, chunk):
    tokens, width = base_ref.shape
    rows = rows_ref.shape[0]
    step = min(256, tokens)
    for start in range(0, tokens, step):
        slots = lax.broadcasted_iota(jnp.int32, (step, rows), 1)
        pick = jnp.where(slots == pos_ref[start : start + step, chunk : chunk + 1], 1.0, 0.0)
        found = jnp.dot(pick.astype(bf16), rows_ref[...], preferred_element_type=f32)
        base = base_ref[start : start + step, :].astype(f32)
        out_ref[start : start + step, :] = (base + found).astype(bf16)


def combine(pos_col, base, rows, chunk):
    return pl.pallas_call(
        functools.partial(combine_kernel, chunk=chunk),
        out_shape=jax.ShapeDtypeStruct(base.shape, bf16),
        in_specs=[whole_vmem()] * 3,
        out_specs=whole_vmem(),
        compiler_params=params(16),
        name="combine",
    )(pos_col, base, rows)


def shards(
    pixels,
    conv_weight,
    norm_gain,
    router_weight,
    gate_weight,
    up_weight,
    down_weight,
    expert_ids,
    neighbours,
):
    tokens, width = pixels.shape
    experts = lax.axis_size("expert")
    parts = lax.axis_size("hidden")
    capacity = max(2, 2 * tokens // experts)
    chunks = CHUNKS
    size = capacity // chunks
    own = lax.axis_index("hidden").astype(jnp.int32).reshape(1)
    far = [(i, i ^ 2) for i in range(parts)]
    near = [(i, i ^ 1) for i in range(parts)]

    def exchange(rows):
        return lax.all_to_all(
            rows.reshape(experts, -1, width), "expert", split_axis=0, concat_axis=0, tiled=True
        )

    ids_row = expert_ids.reshape(1, tokens)
    rim = exchange(rim_send(neighbours, pixels, experts))
    if capacity - 4 * (SIDE - 1) >= size:
        positions, first_rows = early(ids_row, pixels, conv_weight, experts, capacity, chunks)
        conv_out, *later_rows = late(
            neighbours, positions, pixels, conv_weight, rim, 1, experts * size
        )
        sends = [first_rows] + list(later_rows)
    else:
        positions = route_only(ids_row, experts, capacity, chunks)
        conv_out, *sends = late(neighbours, positions, pixels, conv_weight, rim, 0, experts * size)
    pos_col = positions.T
    gain = norm_gain.reshape(parts, 1, width)
    router = router_weight.astype(f32).reshape(parts, 1, width)

    results = []
    for rows in sends:
        mine = exchange(rows).reshape(experts * size, width)
        across = lax.ppermute(mine, "hidden", far)
        beside = lax.ppermute(mine, "hidden", near)
        both = lax.ppermute(across, "hidden", near)
        results.append(
            expert_layer(
                own,
                (mine, across, beside, both),
                gain,
                router,
                gate_weight,
                up_weight,
                down_weight,
            )
        )
    base = conv_out
    for chunk, (keep0, keep1, give) in enumerate(results):
        got = lax.ppermute(give, "hidden", near)
        onward = (keep1.astype(f32) + got[1].astype(f32)).astype(bf16)
        arrived = lax.ppermute(onward, "hidden", far)
        total = (keep0.astype(f32) + got[0].astype(f32) + arrived.astype(f32)).astype(bf16)
        base = combine(pos_col, base, exchange(total).reshape(experts * size, width), chunk)
    return base


def solution(mesh):
    in_specs = (
        P("expert", "hidden"),
        P(None, "hidden"),
        P(),
        P(None, "expert"),
        P("expert", None, "hidden"),
        P("expert", None, "hidden"),
        P("expert", "hidden", None),
        P("expert", None),
        P("expert", None),
    )
    out_specs = P("expert", "hidden")
    return jax.shard_map(shards, mesh=mesh, in_specs=in_specs, out_specs=out_specs, check_vma=False)
```

```python
import functools

import jax
import jax.numpy as jnp
from jax import lax
from jax.experimental import pallas as pl
from jax.experimental.pallas import tpu as pltpu
from jax.sharding import PartitionSpec as P


SIDE = 32
EPSILON = 1e-05
SHARES = (7, 5, 4)
SPLITS = (1, 1, 1)
EXPERT_MIB = 60
LATE_MIB = 24
STRIP = 512

f32 = jnp.float32
bf16 = jnp.bfloat16

SMEM = pltpu.MemorySpace.SMEM


def in_hbm():
    return pl.BlockSpec(memory_space=pltpu.MemorySpace.HBM)


def whole_smem():
    return pl.BlockSpec(memory_space=SMEM)


def params(mib):
    return pltpu.CompilerParams(vmem_limit_bytes=mib << 20)


def put_rim(nbr_ref, pix_ref, out_ref, base):
    tokens = pix_ref.shape[0]
    last = tokens - SIDE
    line = lax.broadcasted_iota(jnp.int32, (2 * SIDE, tokens), 0)
    pixel = lax.broadcasted_iota(jnp.int32, (2 * SIDE, tokens), 1)
    wanted = jnp.where(line < SIDE, line * SIDE, (line - SIDE) * SIDE + SIDE - 1)
    pick = jnp.where(pixel == wanted, 1.0, 0.0).astype(bf16)
    columns = jnp.dot(pick, pix_ref[...], preferred_element_type=f32)
    out_ref[:, base : base + SIDE, :] = jnp.zeros(
        (out_ref.shape[0], SIDE, out_ref.shape[2]), bf16
    )

    def put(direction, piece):
        target = nbr_ref[0, direction]

        @pl.when(target >= 0)
        def _():
            out_ref[jnp.maximum(target, 0), base : base + piece.shape[0], :] = piece

    put(0, pix_ref[:SIDE])
    put(1, pix_ref[last:])
    put(2, columns[:SIDE].astype(bf16))
    put(3, columns[SIDE:].astype(bf16))
    for direction, row in ((4, 0), (5, SIDE), (6, SIDE - 1), (7, 2 * SIDE - 1)):
        corner = columns[row : row + 1, :]
        put(direction, jnp.broadcast_to(corner, (16, corner.shape[1])).astype(bf16))


def rim_kernel(nbr_ref, pix_ref, out_ref):
    put_rim(nbr_ref, pix_ref, out_ref, 0)


def rim_send(neighbours, pixels, experts):
    return pl.pallas_call(
        rim_kernel,
        out_shape=jax.ShapeDtypeStruct((experts, SIDE, pixels.shape[1]), bf16),
        in_specs=[whole_smem(), pl.BlockSpec()],
        compiler_params=params(8),
        name="rim_send",
    )(neighbours, pixels)


def shifted_rows(pix_ref, side_ref):
    tokens = pix_ref.shape[0]
    wide = pix_ref[...].astype(f32)
    side_ref[1, SIDE : SIDE + tokens, :] = wide
    side_ref[0, SIDE : SIDE + tokens, :] = pltpu.roll(wide, 1, 0)
    side_ref[2, SIDE : SIDE + tokens, :] = pltpu.roll(wide, tokens - 1, 0)


def conv_rows(side_ref, weight_ref, conv_ref):
    tokens = conv_ref.shape[0]
    step = 64

    def block(number, carry):
        start = pl.multiple_of(number * step, step)
        total = side_ref[1, pl.ds(start + SIDE, step), :]
        for a in range(3):
            for b in range(3):
                total = (
                    total
                    + weight_ref[3 * a + b : 3 * a + b + 1, :]
                    * side_ref[b, pl.ds(start + SIDE * a, step), :]
                )
        conv_ref[pl.ds(start, step), :] = total.astype(bf16)
        return carry

    lax.fori_loop(0, tokens // step, block, 0)


def send_rows(pos_row, conv, out_ref):
    experts, size = out_ref.shape[0], out_ref.shape[1]
    tokens = conv.shape[0]
    group = max(1, min(experts, 256 // size))
    while experts % group:
        group -= 1
    for first in range(0, experts, group):
        slots = lax.broadcasted_iota(jnp.int32, (group * size, tokens), 0) + first * size
        pick = jnp.where(slots == pos_row, 1.0, 0.0).astype(bf16)
        rows = jnp.dot(pick, conv, preferred_element_type=f32).astype(bf16)
        for number in range(group):
            out_ref[first + number] = rows[number * size : (number + 1) * size]


def route(ids_row, experts, capacity, sizes, split_border):
    tokens = ids_row.shape[1]
    token = lax.broadcasted_iota(jnp.int32, (1, tokens), 1)
    if split_border:
        i, j = token // SIDE, token % SIDE
        border = (i == 0) | (i == SIDE - 1) | (j == 0) | (j == SIDE - 1)
        kind = jnp.where(border, ids_row + experts, ids_row)
        kinds = 2 * experts
    else:
        kind, kinds = ids_row, experts
    onehot = jnp.where(lax.broadcasted_iota(jnp.int32, (kinds, tokens), 0) == kind, 1.0, 0.0)
    before = jnp.where(
        lax.broadcasted_iota(jnp.int32, (tokens, tokens), 0)
        < lax.broadcasted_iota(jnp.int32, (tokens, tokens), 1),
        1.0,
        0.0,
    ).astype(bf16)
    earlier = jnp.dot(onehot.astype(bf16), before, preferred_element_type=f32)
    slot = jnp.sum(onehot * earlier, axis=0, keepdims=True).astype(jnp.int32)
    if split_border:
        slot = jnp.where(border, capacity - 1 - slot, slot)
    result = []
    low = 0
    for size in sizes:
        inside = (slot >= low) & (slot < low + size)
        result.append(jnp.where(inside, ids_row * size + slot - low, -1))
        low += size
    return result


def early_kernel(
    nbr_hbm,
    ids_hbm,
    pix_hbm,
    weight_hbm,
    pos_ref,
    out_ref,
    nbr_ref,
    ids_ref,
    pix_ref,
    weight_ref,
    sems,
    side_ref,
    conv_ref,
    *,
    experts,
    capacity,
    sizes,
):
    loads = [
        pltpu.make_async_copy(source, target, sems.at[number])
        for number, (source, target) in enumerate(
            (
                (ids_hbm, ids_ref),
                (pix_hbm, pix_ref),
                (nbr_hbm, nbr_ref),
                (weight_hbm, weight_ref),
            )
        )
    ]
    for load in loads:
        load.start()
    loads[0].wait()
    positions = route(ids_ref[...], experts, capacity, sizes, True)
    for chunk, position in enumerate(positions):
        pos_ref[chunk : chunk + 1, :] = position
    for load in loads[1:]:
        load.wait()
    put_rim(nbr_ref, pix_ref, out_ref, sizes[0])
    tokens, width = pix_ref.shape
    shifted_rows(pix_ref, side_ref)
    for b in range(3):
        side_ref[b, :SIDE, :] = jnp.zeros((SIDE, width), f32)
        side_ref[b, SIDE + tokens :, :] = jnp.zeros((SIDE, width), f32)
    conv_rows(side_ref, weight_ref, conv_ref)
    send_rows(positions[0], conv_ref[...], out_ref.at[:, : sizes[0], :])


def early(neighbours, ids_row, pixels, conv_weight, experts, capacity, sizes):
    tokens, width = pixels.shape
    return pl.pallas_call(
        functools.partial(early_kernel, experts=experts, capacity=capacity, sizes=sizes),
        out_shape=(
            jax.ShapeDtypeStruct((len(sizes), tokens), jnp.int32),
            jax.ShapeDtypeStruct((experts, sizes[0] + SIDE, width), bf16),
        ),
        in_specs=[in_hbm()] * 4,
        scratch_shapes=[
            pltpu.SMEM(neighbours.shape, jnp.int32),
            pltpu.VMEM(ids_row.shape, jnp.int32),
            pltpu.VMEM(pixels.shape, bf16),
            pltpu.VMEM(conv_weight.shape, f32),
            pltpu.SemaphoreType.DMA((4,)),
            pltpu.VMEM((3, tokens + 2 * SIDE, width), f32),
            pltpu.VMEM((tokens, width), bf16),
        ],
        compiler_params=params(64),
        name="early",
    )(neighbours, ids_row, pixels, conv_weight)


def route_kernel(ids_ref, pos_ref, *, experts, capacity, sizes):
    positions = route(ids_ref[...], experts, capacity, sizes, False)
    for chunk, position in enumerate(positions):
        pos_ref[chunk : chunk + 1, :] = position


def route_only(ids_row, experts, capacity, sizes):
    return pl.pallas_call(
        functools.partial(route_kernel, experts=experts, capacity=capacity, sizes=sizes),
        out_shape=jax.ShapeDtypeStruct((len(sizes), ids_row.shape[1]), jnp.int32),
        compiler_params=params(16),
        name="route",
    )(ids_row)


def late_kernel(
    nbr_hbm, pos_ref, pix_hbm, weight_hbm, rim_ref, conv_ref, *rest, first, base
):
    outs = rest[:-5]
    nbr_ref, pix_ref, weight_ref, sems, side_ref = rest[-5:]
    loads = [
        pltpu.make_async_copy(source, target, sems.at[number])
        for number, (source, target) in enumerate(
            ((nbr_hbm, nbr_ref), (pix_hbm, pix_ref), (weight_hbm, weight_ref))
        )
    ]
    for load in loads:
        load.start()
    for load in loads:
        load.wait()
    tokens, width = pix_ref.shape
    shifted_rows(pix_ref, side_ref)

    def fetch(direction):
        source = nbr_ref[0, direction]
        block = rim_ref[jnp.maximum(source, 0), base : base + SIDE, :].astype(f32)
        return jnp.where(source >= 0, block, 0.0)

    pixel = lax.broadcasted_iota(jnp.int32, (tokens, SIDE), 0)
    line = lax.broadcasted_iota(jnp.int32, (tokens, SIDE), 1)
    column = lax.broadcasted_iota(jnp.int32, (tokens, width), 0) % SIDE
    for b, direction, edge in ((0, 2, 0), (2, 3, SIDE - 1)):
        place = jnp.where(pixel == line * SIDE + edge, 1.0, 0.0).astype(bf16)
        values = jnp.dot(place, fetch(direction).astype(bf16), preferred_element_type=f32)
        inner = side_ref[b, SIDE : SIDE + tokens, :]
        side_ref[b, SIDE : SIDE + tokens, :] = jnp.where(column == edge, values, inner)
    place = lax.broadcasted_iota(jnp.int32, (SIDE, width), 0)
    for middle, left, right, start in ((0, 4, 5, 0), (1, 6, 7, SIDE + tokens)):
        row = fetch(middle)
        side_ref[1, start : start + SIDE, :] = row
        side_ref[0, start : start + SIDE, :] = jnp.where(
            place == 0, fetch(left)[0:1, :], pltpu.roll(row, 1, 0)
        )
        side_ref[2, start : start + SIDE, :] = jnp.where(
            place == SIDE - 1, fetch(right)[0:1, :], pltpu.roll(row, SIDE - 1, 0)
        )
    conv_rows(side_ref, weight_ref, conv_ref)
    for number, out_ref in enumerate(outs):
        chunk = first + number
        send_rows(pos_ref[chunk : chunk + 1, :], conv_ref[...], out_ref)


def late(neighbours, positions, pixels, conv_weight, rim, experts, first, sizes):
    tokens, width = pixels.shape
    outs = (jax.ShapeDtypeStruct((tokens, width), bf16),) + tuple(
        jax.ShapeDtypeStruct((experts, size, width), bf16) for size in sizes[first:]
    )
    base = sizes[0] if first else 0
    return pl.pallas_call(
        functools.partial(late_kernel, first=first, base=base),
        out_shape=outs,
        in_specs=[in_hbm(), pl.BlockSpec(), in_hbm(), in_hbm(), pl.BlockSpec()],
        scratch_shapes=[
            pltpu.SMEM(neighbours.shape, jnp.int32),
            pltpu.VMEM(pixels.shape, bf16),
            pltpu.VMEM(conv_weight.shape, f32),
            pltpu.SemaphoreType.DMA((3,)),
            pltpu.VMEM((3, tokens + 2 * SIDE, width), f32),
        ],
        compiler_params=params(LATE_MIB),
        name="late",
    )(neighbours, positions, pixels, conv_weight, rim)


def expert_kernel(
    own_ref,
    x0_hbm,
    x1_hbm,
    x2_hbm,
    x3_hbm,
    gain_ref,
    router_ref,
    gate_hbm,
    up_hbm,
    down_hbm,
    keep0_ref,
    keep1_ref,
    give_ref,
    x_ref,
    normed_ref,
    hidden_ref,
    gate_ref,
    up_ref,
    down_ref,
    x_sems,
    w_sems,
    *,
    step,
    places,
):
    own = own_ref[0]
    order = (own, own ^ 2, own ^ 1, own ^ 3)
    parts, total, width = x_ref.shape
    strips = hidden_ref.shape[1] // STRIP
    starts = range(0, total, step)

    def columns(part):
        return pl.ds(pl.multiple_of(part * width, width), width)

    x_loads = [
        [
            pltpu.make_async_copy(
                source.at[pl.ds(place * total + start, step), :],
                x_ref.at[part, pl.ds(start, step), :],
                x_sems.at[block, part],
            )
            for part, (source, place) in enumerate(zip((x0_hbm, x1_hbm, x2_hbm, x3_hbm), places))
        ]
        for block, start in enumerate(starts)
    ]
    w_loads = []
    for strip in range(strips):
        here = pl.ds(strip * STRIP, STRIP)
        for source, target in ((gate_hbm, gate_ref), (up_hbm, up_ref)):
            w_loads.append(
                pltpu.make_async_copy(
                    source.at[0, :, here], target.at[strip], w_sems.at[len(w_loads)]
                )
            )
    down_load = pltpu.make_async_copy(down_hbm.at[0], down_ref, w_sems.at[len(w_loads)])
    for load in x_loads[0] + w_loads[:2]:
        load.start()
    for loads in x_loads[1:]:
        for load in loads:
            load.start()
    for load in w_loads[2:] + [down_load]:
        load.start()

    weights = []
    for strip in range(strips):
        for block, start in enumerate(starts):
            here = slice(start, start + step)
            if strip == 0:
                for load in x_loads[block]:
                    load.wait()
                square = 0.0
                for part in range(parts):
                    wide = x_ref[part, here, :].astype(f32)
                    square = square + wide * wide
                mean_sq = jnp.sum(square, axis=1, keepdims=True) * (1.0 / (width * parts))
                scale = lax.rsqrt(mean_sq + EPSILON)
                score = 0.0
                for part, place in enumerate(order):
                    wide = x_ref[part, here, :].astype(f32)
                    normed = (wide * scale * gain_ref[place]).astype(bf16)
                    score = score + normed.astype(f32) * router_ref[place]
                    normed_ref[here, columns(place)] = normed
                weights.append(jax.nn.sigmoid(jnp.sum(score, axis=1, keepdims=True)))
            rows = normed_ref[here, :]
            if block == 0:
                w_loads[2 * strip].wait()
            gate = jnp.dot(rows, gate_ref[strip], preferred_element_type=f32)
            if block == 0:
                w_loads[2 * strip + 1].wait()
            up = jnp.dot(rows, up_ref[strip], preferred_element_type=f32)
            hidden = gate / (1.0 + jnp.exp(-gate)) * up * weights[block]
            hidden_ref[here, strip * STRIP : (strip + 1) * STRIP] = hidden.astype(bf16)
    down_load.wait()
    for start in starts:
        here = slice(start, start + step)
        rows = hidden_ref[here, :]
        for target, part in zip((keep0_ref, keep1_ref, give_ref.at[0], give_ref.at[1]), order):
            target[here, :] = jnp.dot(
                rows, down_ref[:, columns(part)], preferred_element_type=f32
            ).astype(bf16)


def expert_layer(own, pieces, places, rows, gain, router, gate_weight, up_weight, down_weight):
    width = pieces[0].shape[1]
    full, units = gate_weight.shape[1:]
    step = next(n for n in (256, 192, 128, 64, 32, 16, 8) if rows % n == 0)
    blocks = rows // step
    parts = len(pieces)
    return pl.pallas_call(
        functools.partial(expert_kernel, step=step, places=places),
        out_shape=(
            jax.ShapeDtypeStruct((rows, width), bf16),
            jax.ShapeDtypeStruct((rows, width), bf16),
            jax.ShapeDtypeStruct((2, rows, width), bf16),
        ),
        in_specs=[whole_smem()]
        + [in_hbm()] * parts
        + [pl.BlockSpec(), pl.BlockSpec()]
        + [in_hbm()] * 3,
        scratch_shapes=[
            pltpu.VMEM((parts, rows, width), bf16),
            pltpu.VMEM((rows, full), bf16),
            pltpu.VMEM((rows, units), bf16),
            pltpu.VMEM((units // STRIP, full, STRIP), bf16),
            pltpu.VMEM((units // STRIP, full, STRIP), bf16),
            pltpu.VMEM((units, full), bf16),
            pltpu.SemaphoreType.DMA((blocks, parts)),
            pltpu.SemaphoreType.DMA((2 * units // STRIP + 1,)),
        ],
        compiler_params=params(EXPERT_MIB),
        cost_estimate=pl.CostEstimate(
            flops=6 * rows * full * units,
            transcendentals=rows * units,
            bytes_accessed=3 * 2 * full * units + 4 * rows * full,
        ),
        name="expert",
    )(own, *pieces, gain, router, gate_weight, up_weight, down_weight)


def combine_kernel(pos_ref, base_ref, rows_ref, out_ref, *, chunk):
    tokens, _ = base_ref.shape
    rows = rows_ref.shape[0]
    step = min(256, tokens)
    for start in range(0, tokens, step):
        slots = lax.broadcasted_iota(jnp.int32, (step, rows), 1)
        pick = jnp.where(slots == pos_ref[start : start + step, chunk : chunk + 1], 1.0, 0.0)
        found = jnp.dot(pick.astype(bf16), rows_ref[...], preferred_element_type=f32)
        base = base_ref[start : start + step, :].astype(f32)
        out_ref[start : start + step, :] = (base + found).astype(bf16)


def combine(pos_col, base, rows, chunk):
    return pl.pallas_call(
        functools.partial(combine_kernel, chunk=chunk),
        out_shape=jax.ShapeDtypeStruct(base.shape, bf16),
        compiler_params=params(16),
        name="combine",
    )(pos_col, base, rows)


def shards(
    pixels,
    conv_weight,
    norm_gain,
    router_weight,
    gate_weight,
    up_weight,
    down_weight,
    expert_ids,
    neighbours,
):
    tokens, width = pixels.shape
    experts = lax.axis_size("expert")
    parts = lax.axis_size("hidden")
    capacity = max(2, 2 * tokens // experts)
    sizes = tuple(share * capacity // sum(SHARES) for share in SHARES)
    own = lax.axis_index("hidden").astype(jnp.int32).reshape(1)
    far = [(i, i ^ 2) for i in range(parts)]
    near = [(i, i ^ 1) for i in range(parts)]

    def exchange(rows):
        return lax.all_to_all(rows, "expert", split_axis=0, concat_axis=0, tiled=True)

    ids_row = expert_ids.reshape(1, tokens)
    arrived = []
    if capacity - 4 * (SIDE - 1) >= sizes[0]:
        positions, sent = early(
            neighbours, ids_row, pixels, conv_weight, experts, capacity, sizes
        )
        rim = exchange(sent)
        arrived.append(rim[:, : sizes[0]])
    else:
        positions = route_only(ids_row, experts, capacity, sizes)
        rim = exchange(rim_send(neighbours, pixels, experts))
    first = len(arrived)
    conv_out, *sends = late(neighbours, positions, pixels, conv_weight, rim, experts, first, sizes)
    for sent in sends:
        arrived.append(exchange(sent))
    gain = norm_gain.reshape(parts, 1, width)
    router = router_weight.astype(f32).reshape(parts, 1, width)

    ready = []
    for chunk, rows in enumerate(arrived):
        mine = rows.reshape(-1, width)
        count = mine.shape[0] // SPLITS[chunk]
        beside = lax.ppermute(mine, "hidden", near)
        whole = []
        for split in range(SPLITS[chunk]):
            across = lax.ppermute(
                mine[split * count : (split + 1) * count], "hidden", far
            )
            both = lax.ppermute(across, "hidden", near)
            keep0, keep1, give = expert_layer(
                own,
                (mine, across, beside, both),
                (split, 0, split, 0),
                count,
                gain,
                router,
                gate_weight,
                up_weight,
                down_weight,
            )
            got = lax.ppermute(give, "hidden", near)
            onward = (keep1.astype(f32) + got[1].astype(f32)).astype(bf16)
            last = lax.ppermute(onward, "hidden", far)
            whole.append(
                (keep0.astype(f32) + got[0].astype(f32) + last.astype(f32)).astype(bf16)
            )
        ready.append(jnp.concatenate(whole, axis=0) if len(whole) > 1 else whole[0])
    base = conv_out
    pos_col = positions.T
    for chunk, rows in enumerate(ready):
        back = exchange(rows.reshape(experts, sizes[chunk], width))
        base = combine(pos_col, base, back.reshape(-1, width), chunk)
    return base


def solution(mesh):
    in_specs = (
        P("expert", "hidden"),
        P(None, "hidden"),
        P(),
        P(None, "expert"),
        P("expert", None, "hidden"),
        P("expert", None, "hidden"),
        P("expert", "hidden", None),
        P("expert", None),
        P("expert", None),
    )
    out_specs = P("expert", "hidden")
    return jax.shard_map(shards, mesh=mesh, in_specs=in_specs, out_specs=out_specs, check_vma=False)
```

```python
import functools

import jax
import jax.numpy as jnp
from jax import lax
from jax.experimental import pallas as pl
from jax.experimental.pallas import tpu as pltpu
from jax.sharding import PartitionSpec as P


SIDE = 32
EPSILON = 1e-05
SHARES = (7, 5, 4)
SPLITS = (1, 1, 1)
EXPERT_MIB = 60
LATE_MIB = 24
STRIP = 512

f32 = jnp.float32
bf16 = jnp.bfloat16

SMEM = pltpu.MemorySpace.SMEM


def in_hbm():
    return pl.BlockSpec(memory_space=pltpu.MemorySpace.HBM)


def whole_smem():
    return pl.BlockSpec(memory_space=SMEM)


def params(mib):
    return pltpu.CompilerParams(vmem_limit_bytes=mib << 20)


def put_rim(nbr_ref, pix_ref, out_ref, base):
    tokens = pix_ref.shape[0]
    last = tokens - SIDE
    line = lax.broadcasted_iota(jnp.int32, (2 * SIDE, tokens), 0)
    pixel = lax.broadcasted_iota(jnp.int32, (2 * SIDE, tokens), 1)
    wanted = jnp.where(line < SIDE, line * SIDE, (line - SIDE) * SIDE + SIDE - 1)
    pick = jnp.where(pixel == wanted, 1.0, 0.0).astype(bf16)
    columns = jnp.dot(pick, pix_ref[...], preferred_element_type=f32)
    out_ref[:, base : base + SIDE, :] = jnp.zeros(
        (out_ref.shape[0], SIDE, out_ref.shape[2]), bf16
    )

    def put(direction, piece):
        target = nbr_ref[0, direction]

        @pl.when(target >= 0)
        def _():
            out_ref[jnp.maximum(target, 0), base : base + piece.shape[0], :] = piece

    put(0, pix_ref[:SIDE])
    put(1, pix_ref[last:])
    put(2, columns[:SIDE].astype(bf16))
    put(3, columns[SIDE:].astype(bf16))
    for direction, row in ((4, 0), (5, SIDE), (6, SIDE - 1), (7, 2 * SIDE - 1)):
        corner = columns[row : row + 1, :]
        put(direction, jnp.broadcast_to(corner, (16, corner.shape[1])).astype(bf16))


def rim_kernel(nbr_ref, pix_ref, out_ref):
    put_rim(nbr_ref, pix_ref, out_ref, 0)


def rim_send(neighbours, pixels, experts):
    return pl.pallas_call(
        rim_kernel,
        out_shape=jax.ShapeDtypeStruct((experts, SIDE, pixels.shape[1]), bf16),
        in_specs=[whole_smem(), pl.BlockSpec()],
        compiler_params=params(8),
        name="rim_send",
    )(neighbours, pixels)


def shifted_rows(pix_ref, side_ref):
    tokens = pix_ref.shape[0]
    wide = pix_ref[...].astype(f32)
    side_ref[1, SIDE : SIDE + tokens, :] = wide
    side_ref[0, SIDE : SIDE + tokens, :] = pltpu.roll(wide, 1, 0)
    side_ref[2, SIDE : SIDE + tokens, :] = pltpu.roll(wide, tokens - 1, 0)


def conv_rows(side_ref, weight_ref, conv_ref):
    tokens = conv_ref.shape[0]
    step = 64

    def block(number, carry):
        start = pl.multiple_of(number * step, step)
        total = side_ref[1, pl.ds(start + SIDE, step), :]
        for a in range(3):
            for b in range(3):
                total = (
                    total
                    + weight_ref[3 * a + b : 3 * a + b + 1, :]
                    * side_ref[b, pl.ds(start + SIDE * a, step), :]
                )
        conv_ref[pl.ds(start, step), :] = total.astype(bf16)
        return carry

    lax.fori_loop(0, tokens // step, block, 0)


def send_rows(pos_row, conv, out_ref):
    experts, size = out_ref.shape[0], out_ref.shape[1]
    tokens = conv.shape[0]
    group = max(1, min(experts, 256 // size))
    while experts % group:
        group -= 1
    for first in range(0, experts, group):
        slots = lax.broadcasted_iota(jnp.int32, (group * size, tokens), 0) + first * size
        pick = jnp.where(slots == pos_row, 1.0, 0.0).astype(bf16)
        rows = jnp.dot(pick, conv, preferred_element_type=f32).astype(bf16)
        for number in range(group):
            out_ref[first + number] = rows[number * size : (number + 1) * size]


def route(ids_row, experts, capacity, sizes, split_border):
    tokens = ids_row.shape[1]
    token = lax.broadcasted_iota(jnp.int32, (1, tokens), 1)
    if split_border:
        i, j = token // SIDE, token % SIDE
        border = (i == 0) | (i == SIDE - 1) | (j == 0) | (j == SIDE - 1)
        kind = jnp.where(border, ids_row + experts, ids_row)
        kinds = 2 * experts
    else:
        kind, kinds = ids_row, experts
    onehot = jnp.where(lax.broadcasted_iota(jnp.int32, (kinds, tokens), 0) == kind, 1.0, 0.0)
    before = jnp.where(
        lax.broadcasted_iota(jnp.int32, (tokens, tokens), 0)
        < lax.broadcasted_iota(jnp.int32, (tokens, tokens), 1),
        1.0,
        0.0,
    ).astype(bf16)
    earlier = jnp.dot(onehot.astype(bf16), before, preferred_element_type=f32)
    slot = jnp.sum(onehot * earlier, axis=0, keepdims=True).astype(jnp.int32)
    if split_border:
        slot = jnp.where(border, capacity - 1 - slot, slot)
    result = []
    low = 0
    for size in sizes:
        inside = (slot >= low) & (slot < low + size)
        result.append(jnp.where(inside, ids_row * size + slot - low, -1))
        low += size
    return result


def early_kernel(
    nbr_hbm,
    ids_hbm,
    pix_hbm,
    weight_hbm,
    pos_ref,
    out_ref,
    nbr_ref,
    ids_ref,
    pix_ref,
    weight_ref,
    sems,
    side_ref,
    conv_ref,
    *,
    experts,
    capacity,
    sizes,
):
    loads = [
        pltpu.make_async_copy(source, target, sems.at[number])
        for number, (source, target) in enumerate(
            (
                (ids_hbm, ids_ref),
                (pix_hbm, pix_ref),
                (nbr_hbm, nbr_ref),
                (weight_hbm, weight_ref),
            )
        )
    ]
    for load in loads:
        load.start()
    loads[0].wait()
    positions = route(ids_ref[...], experts, capacity, sizes, True)
    for chunk, position in enumerate(positions):
        pos_ref[chunk : chunk + 1, :] = position
    for load in loads[1:]:
        load.wait()
    put_rim(nbr_ref, pix_ref, out_ref, sizes[0])
    tokens, width = pix_ref.shape
    shifted_rows(pix_ref, side_ref)
    for b in range(3):
        side_ref[b, :SIDE, :] = jnp.zeros((SIDE, width), f32)
        side_ref[b, SIDE + tokens :, :] = jnp.zeros((SIDE, width), f32)
    conv_rows(side_ref, weight_ref, conv_ref)
    send_rows(positions[0], conv_ref[...], out_ref.at[:, : sizes[0], :])


def early(neighbours, ids_row, pixels, conv_weight, experts, capacity, sizes):
    tokens, width = pixels.shape
    return pl.pallas_call(
        functools.partial(early_kernel, experts=experts, capacity=capacity, sizes=sizes),
        out_shape=(
            jax.ShapeDtypeStruct((len(sizes), tokens), jnp.int32),
            jax.ShapeDtypeStruct((experts, sizes[0] + SIDE, width), bf16),
        ),
        in_specs=[in_hbm()] * 4,
        scratch_shapes=[
            pltpu.SMEM(neighbours.shape, jnp.int32),
            pltpu.VMEM(ids_row.shape, jnp.int32),
            pltpu.VMEM(pixels.shape, bf16),
            pltpu.VMEM(conv_weight.shape, f32),
            pltpu.SemaphoreType.DMA((4,)),
            pltpu.VMEM((3, tokens + 2 * SIDE, width), f32),
            pltpu.VMEM((tokens, width), bf16),
        ],
        compiler_params=params(64),
        name="early",
    )(neighbours, ids_row, pixels, conv_weight)


def route_kernel(ids_ref, pos_ref, *, experts, capacity, sizes):
    positions = route(ids_ref[...], experts, capacity, sizes, False)
    for chunk, position in enumerate(positions):
        pos_ref[chunk : chunk + 1, :] = position


def route_only(ids_row, experts, capacity, sizes):
    return pl.pallas_call(
        functools.partial(route_kernel, experts=experts, capacity=capacity, sizes=sizes),
        out_shape=jax.ShapeDtypeStruct((len(sizes), ids_row.shape[1]), jnp.int32),
        compiler_params=params(16),
        name="route",
    )(ids_row)


def late_kernel(
    nbr_hbm, pos_ref, pix_hbm, weight_hbm, rim_ref, conv_ref, *rest, first, base
):
    outs = rest[:-5]
    nbr_ref, pix_ref, weight_ref, sems, side_ref = rest[-5:]
    loads = [
        pltpu.make_async_copy(source, target, sems.at[number])
        for number, (source, target) in enumerate(
            ((nbr_hbm, nbr_ref), (pix_hbm, pix_ref), (weight_hbm, weight_ref))
        )
    ]
    for load in loads:
        load.start()
    for load in loads:
        load.wait()
    tokens, width = pix_ref.shape
    shifted_rows(pix_ref, side_ref)

    def fetch(direction):
        source = nbr_ref[0, direction]
        block = rim_ref[jnp.maximum(source, 0), base : base + SIDE, :].astype(f32)
        return jnp.where(source >= 0, block, 0.0)

    pixel = lax.broadcasted_iota(jnp.int32, (tokens, SIDE), 0)
    line = lax.broadcasted_iota(jnp.int32, (tokens, SIDE), 1)
    column = lax.broadcasted_iota(jnp.int32, (tokens, width), 0) % SIDE
    for b, direction, edge in ((0, 2, 0), (2, 3, SIDE - 1)):
        place = jnp.where(pixel == line * SIDE + edge, 1.0, 0.0).astype(bf16)
        values = jnp.dot(place, fetch(direction).astype(bf16), preferred_element_type=f32)
        inner = side_ref[b, SIDE : SIDE + tokens, :]
        side_ref[b, SIDE : SIDE + tokens, :] = jnp.where(column == edge, values, inner)
    place = lax.broadcasted_iota(jnp.int32, (SIDE, width), 0)
    for middle, left, right, start in ((0, 4, 5, 0), (1, 6, 7, SIDE + tokens)):
        row = fetch(middle)
        side_ref[1, start : start + SIDE, :] = row
        side_ref[0, start : start + SIDE, :] = jnp.where(
            place == 0, fetch(left)[0:1, :], pltpu.roll(row, 1, 0)
        )
        side_ref[2, start : start + SIDE, :] = jnp.where(
            place == SIDE - 1, fetch(right)[0:1, :], pltpu.roll(row, SIDE - 1, 0)
        )
    conv_rows(side_ref, weight_ref, conv_ref)
    for number, out_ref in enumerate(outs):
        chunk = first + number
        send_rows(pos_ref[chunk : chunk + 1, :], conv_ref[...], out_ref)


def late(neighbours, positions, pixels, conv_weight, rim, experts, first, sizes):
    tokens, width = pixels.shape
    outs = (jax.ShapeDtypeStruct((tokens, width), bf16),) + tuple(
        jax.ShapeDtypeStruct((experts, size, width), bf16) for size in sizes[first:]
    )
    base = sizes[0] if first else 0
    return pl.pallas_call(
        functools.partial(late_kernel, first=first, base=base),
        out_shape=outs,
        in_specs=[in_hbm(), pl.BlockSpec(), in_hbm(), in_hbm(), pl.BlockSpec()],
        scratch_shapes=[
            pltpu.SMEM(neighbours.shape, jnp.int32),
            pltpu.VMEM(pixels.shape, bf16),
            pltpu.VMEM(conv_weight.shape, f32),
            pltpu.SemaphoreType.DMA((3,)),
            pltpu.VMEM((3, tokens + 2 * SIDE, width), f32),
        ],
        compiler_params=params(LATE_MIB),
        name="late",
    )(neighbours, positions, pixels, conv_weight, rim)


def expert_kernel(
    own_ref,
    x0_hbm,
    x1_hbm,
    x2_hbm,
    x3_hbm,
    gain_ref,
    router_ref,
    gate_hbm,
    up_hbm,
    down_hbm,
    keep0_ref,
    keep1_ref,
    give0_ref,
    give1_ref,
    x_ref,
    normed_ref,
    hidden_ref,
    gate_ref,
    up_ref,
    down_ref,
    x_sems,
    w_sems,
    *,
    step,
    places,
):
    own = own_ref[0]
    order = (own, own ^ 2, own ^ 1, own ^ 3)
    parts, total, width = x_ref.shape
    strips = hidden_ref.shape[1] // STRIP
    starts = range(0, total, step)

    def columns(part):
        return pl.ds(pl.multiple_of(part * width, width), width)

    x_loads = [
        [
            pltpu.make_async_copy(
                source.at[pl.ds(place * total + start, step), :],
                x_ref.at[part, pl.ds(start, step), :],
                x_sems.at[block, part],
            )
            for part, (source, place) in enumerate(zip((x0_hbm, x1_hbm, x2_hbm, x3_hbm), places))
        ]
        for block, start in enumerate(starts)
    ]
    w_loads = []
    for strip in range(strips):
        here = pl.ds(strip * STRIP, STRIP)
        for source, target in ((gate_hbm, gate_ref), (up_hbm, up_ref)):
            w_loads.append(
                pltpu.make_async_copy(
                    source.at[0, :, here], target.at[strip], w_sems.at[len(w_loads)]
                )
            )
    down_load = pltpu.make_async_copy(down_hbm.at[0], down_ref, w_sems.at[len(w_loads)])
    for load in x_loads[0] + w_loads[:2]:
        load.start()
    for loads in x_loads[1:]:
        for load in loads:
            load.start()
    for load in w_loads[2:] + [down_load]:
        load.start()

    weights = []
    for strip in range(strips):
        for block, start in enumerate(starts):
            here = slice(start, start + step)
            if strip == 0:
                for load in x_loads[block]:
                    load.wait()
                square = 0.0
                for part in range(parts):
                    wide = x_ref[part, here, :].astype(f32)
                    square = square + wide * wide
                mean_sq = jnp.sum(square, axis=1, keepdims=True) * (1.0 / (width * parts))
                scale = lax.rsqrt(mean_sq + EPSILON)
                score = 0.0
                for part, place in enumerate(order):
                    wide = x_ref[part, here, :].astype(f32)
                    normed = (wide * scale * gain_ref[place]).astype(bf16)
                    score = score + normed.astype(f32) * router_ref[place]
                    normed_ref[here, columns(place)] = normed
                weights.append(jax.nn.sigmoid(jnp.sum(score, axis=1, keepdims=True)))
            rows = normed_ref[here, :]
            if block == 0:
                w_loads[2 * strip].wait()
            gate = jnp.dot(rows, gate_ref[strip], preferred_element_type=f32)
            if block == 0:
                w_loads[2 * strip + 1].wait()
            up = jnp.dot(rows, up_ref[strip], preferred_element_type=f32)
            hidden = gate / (1.0 + jnp.exp(-gate)) * up * weights[block]
            hidden_ref[here, strip * STRIP : (strip + 1) * STRIP] = hidden.astype(bf16)
    down_load.wait()
    for start in starts:
        here = slice(start, start + step)
        rows = hidden_ref[here, :]
        for target, part in zip((keep0_ref, keep1_ref, give0_ref, give1_ref), order):
            target[here, :] = jnp.dot(
                rows, down_ref[:, columns(part)], preferred_element_type=f32
            ).astype(bf16)


def expert_layer(own, pieces, places, rows, gain, router, gate_weight, up_weight, down_weight):
    width = pieces[0].shape[1]
    full, units = gate_weight.shape[1:]
    step = next(n for n in range(min(320, rows), 0, -8) if rows % n == 0)
    blocks = rows // step
    parts = len(pieces)
    return pl.pallas_call(
        functools.partial(expert_kernel, step=step, places=places),
        out_shape=(jax.ShapeDtypeStruct((rows, width), bf16),) * 4,
        in_specs=[whole_smem()]
        + [in_hbm()] * parts
        + [pl.BlockSpec(), pl.BlockSpec()]
        + [in_hbm()] * 3,
        scratch_shapes=[
            pltpu.VMEM((parts, rows, width), bf16),
            pltpu.VMEM((rows, full), bf16),
            pltpu.VMEM((rows, units), bf16),
            pltpu.VMEM((units // STRIP, full, STRIP), bf16),
            pltpu.VMEM((units // STRIP, full, STRIP), bf16),
            pltpu.VMEM((units, full), bf16),
            pltpu.SemaphoreType.DMA((blocks, parts)),
            pltpu.SemaphoreType.DMA((2 * units // STRIP + 1,)),
        ],
        compiler_params=params(EXPERT_MIB),
        cost_estimate=pl.CostEstimate(
            flops=6 * rows * full * units,
            transcendentals=rows * units,
            bytes_accessed=3 * 2 * full * units + 4 * rows * full,
        ),
        name="expert",
    )(own, *pieces, gain, router, gate_weight, up_weight, down_weight)


def combine_kernel(pos_ref, base_ref, rows_ref, out_ref, *, chunk):
    tokens, _ = base_ref.shape
    rows = rows_ref.shape[0]
    step = min(256, tokens)
    for start in range(0, tokens, step):
        slots = lax.broadcasted_iota(jnp.int32, (step, rows), 1)
        pick = jnp.where(slots == pos_ref[start : start + step, chunk : chunk + 1], 1.0, 0.0)
        found = jnp.dot(pick.astype(bf16), rows_ref[...], preferred_element_type=f32)
        base = base_ref[start : start + step, :].astype(f32)
        out_ref[start : start + step, :] = (base + found).astype(bf16)


def combine(pos_col, base, rows, chunk):
    return pl.pallas_call(
        functools.partial(combine_kernel, chunk=chunk),
        out_shape=jax.ShapeDtypeStruct(base.shape, bf16),
        compiler_params=params(16),
        name="combine",
    )(pos_col, base, rows)


def shards(
    pixels,
    conv_weight,
    norm_gain,
    router_weight,
    gate_weight,
    up_weight,
    down_weight,
    expert_ids,
    neighbours,
):
    tokens, width = pixels.shape
    experts = lax.axis_size("expert")
    parts = lax.axis_size("hidden")
    capacity = max(2, 2 * tokens // experts)
    sizes = tuple(share * capacity // sum(SHARES) for share in SHARES)
    own = lax.axis_index("hidden").astype(jnp.int32).reshape(1)
    far = [(i, i ^ 2) for i in range(parts)]
    near = [(i, i ^ 1) for i in range(parts)]

    def exchange(rows):
        return lax.all_to_all(rows, "expert", split_axis=0, concat_axis=0, tiled=True)

    ids_row = expert_ids.reshape(1, tokens)
    arrived = []
    if capacity - 4 * (SIDE - 1) >= sizes[0]:
        positions, sent = early(
            neighbours, ids_row, pixels, conv_weight, experts, capacity, sizes
        )
        rim = exchange(sent)
        arrived.append(rim[:, : sizes[0]])
    else:
        positions = route_only(ids_row, experts, capacity, sizes)
        rim = exchange(rim_send(neighbours, pixels, experts))
    first = len(arrived)
    conv_out, *sends = late(neighbours, positions, pixels, conv_weight, rim, experts, first, sizes)
    for sent in sends:
        arrived.append(exchange(sent))
    gain = norm_gain.reshape(parts, 1, width)
    router = router_weight.astype(f32).reshape(parts, 1, width)

    ready = []
    for chunk, rows in enumerate(arrived):
        mine = rows.reshape(-1, width)
        count = mine.shape[0] // SPLITS[chunk]
        beside = lax.ppermute(mine, "hidden", near)
        whole = []
        for split in range(SPLITS[chunk]):
            across = lax.ppermute(
                mine[split * count : (split + 1) * count], "hidden", far
            )
            both = lax.ppermute(across, "hidden", near)
            keep0, keep1, give0, give1 = expert_layer(
                own,
                (mine, across, beside, both),
                (split, 0, split, 0),
                count,
                gain,
                router,
                gate_weight,
                up_weight,
                down_weight,
            )
            got1 = lax.ppermute(give1, "hidden", near)
            got0 = lax.ppermute(give0, "hidden", near)
            onward = (keep1.astype(f32) + got1.astype(f32)).astype(bf16)
            last = lax.ppermute(onward, "hidden", far)
            whole.append(
                (keep0.astype(f32) + got0.astype(f32) + last.astype(f32)).astype(bf16)
            )
        ready.append(jnp.concatenate(whole, axis=0) if len(whole) > 1 else whole[0])
    base = conv_out
    pos_col = positions.T
    for chunk, rows in enumerate(ready):
        back = exchange(rows.reshape(experts, sizes[chunk], width))
        base = combine(pos_col, base, back.reshape(-1, width), chunk)
    return base


def solution(mesh):
    in_specs = (
        P("expert", "hidden"),
        P(None, "hidden"),
        P(),
        P(None, "expert"),
        P("expert", None, "hidden"),
        P("expert", None, "hidden"),
        P("expert", "hidden", None),
        P("expert", None),
        P("expert", None),
    )
    out_specs = P("expert", "hidden")
    return jax.shard_map(shards, mesh=mesh, in_specs=in_specs, out_specs=out_specs, check_vma=False)
```
